256 devices in a mesh: pair: 2 (over core), ctx: 4 (over y), vocab: 32 (over z, x).
Axes of the slice: x: 4, y: 4, z: 8, core: 2. Of those that a mesh axis runs over, the one named last changes fastest.
Arguments:
- hidden: bfloat16 [2, 512, 8192], P('pair', 'ctx'), may hold values from -8 to 8
- head_weight: bfloat16 [65536, 8192], P(('ctx', 'vocab'), 'pair'), may hold values from -2 to 2
- labels: int32 [2, 512], P('pair'), may hold values from 0 to 65535
- token_mask: int32 [2, 512], P('pair'), may hold values 0 or 1
- other_logps: float32 [2], P('pair'), may hold values from -780300 to -780000
- ref_logps: float32 [2], P('pair'), may hold values from -781300 to -781000
Outputs:
- grad_hidden: bfloat16 [2, 512, 8192], P(None, 'ctx', ('pair', 'vocab'))
- grad_head: bfloat16 [65536, 8192], P(('ctx', 'vocab'), 'pair')
The draws below stay inside these ranges and needn't reach their ends.
All inputs are finite; a program needn't handle non-finite values. No bound on the sum of `token_mask` on one device may be relied on, other than what follows from the above.
Results may differ from the reference program's by a relative error of at most 0.012.
Values may be sent and summed in bfloat16 or wider, within the bound.
No kernel may reach another device: no remote copies, remote signals or barrier semaphores. Data moves between devices by JAX's collectives and lax.ppermute only.
A program may use at most 128 MiB of HBM per device.

```python
import math
import jax
import jax.numpy as jnp

D = 8192
TOK = 512
V = 65536


def head_table(key):
    normal_draw = jax.random.normal(jax.random.fold_in(key, 7), (V, D), jnp.float32)
    return jnp.clip(normal_draw, -4.0, 4.0) * (3.0 / math.sqrt(D))


def draw_head_weight(key, part):
    return head_table(key).astype(jnp.bfloat16)


def draw_hidden(key, part):
    base = jnp.clip(jax.random.normal(jax.random.fold_in(key, 11), (2, TOK, D), jnp.float32), -6.0, 6.0)
    return jnp.clip(base, -8.0, 8.0).astype(jnp.bfloat16)


def set_ends(drawn, rng, smallest, top_value):
    longest = drawn.shape.index(max(drawn.shape))
    spots = []
    for shift in (0, 1):
        where = [jax.random.randint(jax.random.fold_in(rng, axis), (), 0, length) for axis, length in enumerate(drawn.shape)]
        where[longest] = (where[longest] + shift) % drawn.shape[longest]
        spots.append(tuple(where))
    return drawn.at[spots[0]].set(smallest).at[spots[1]].set(top_value)


def level_of(rng, extent, cuts, least, largest):
    loudness = 1.0
    for dim, parts in cuts:
        steps = jax.random.uniform(jax.random.fold_in(jax.random.fold_in(rng, 6), dim), (parts,), jnp.float32, least / len(cuts), largest / len(cuts))
        loudness = loudness * jnp.repeat(jnp.exp(steps), extent[dim] // parts).reshape((-1,) + (1,) * (len(extent) - 1 - dim))
    return loudness


def setup_inputs(seed: int = 0) -> dict:
    keys = jax.random.split(jax.random.key(seed), 7)
    hidden = draw_hidden(jax.random.fold_in(keys[6], 71), 0)
    head_weight = draw_head_weight(jax.random.fold_in(keys[6], 71), 0)
    labels = set_ends(jax.random.randint(keys[2], (2, TOK), 0, V), jax.random.fold_in(keys[2], 1), 0, V - 1).astype(jnp.int32)
    token_mask = set_ends((jax.random.randint(keys[3], (2, TOK), 0, 4) < 3).astype(jnp.int32), jax.random.fold_in(keys[3], 1), 0, 1)
    other_logps = jnp.clip(-780300.0 + 300.0 * jax.random.uniform(keys[4], (2,), jnp.float32) ** level_of(keys[4], (2,), ((0, 2),), -0.2, 0.2), -780300.0, -780000.0)
    ref_logps = jnp.clip(-781300.0 + 300.0 * jax.random.uniform(keys[5], (2,), jnp.float32) ** level_of(keys[5], (2,), ((0, 2),), -0.2, 0.2), -781300.0, -781000.0)
    return {"hidden": hidden, "head_weight": head_weight, "labels": labels, "token_mask": token_mask, "other_logps": other_logps, "ref_logps": ref_logps}


beta_value = 0.01
z_weight = 0.0001
loss_scale = 4096.0


def reference(hidden, head_weight, labels, token_mask, other_logps, ref_logps):
    logit_list = []
    total_list = []
    label_list = []
    for member in range(2):
        logits = jnp.dot(hidden[member], head_weight.T, preferred_element_type=jnp.float32)
        row_max = jnp.max(logits, axis=1)
        log_total = row_max + jnp.log(jnp.sum(jnp.exp(logits - row_max[:, None]), axis=1))
        label_logit = jnp.take_along_axis(logits, labels[member][:, None], axis=1)[:, 0]
        logit_list.append(logits)
        total_list.append(log_total)
        label_list.append(label_logit)
    maskf = token_mask.astype(jnp.float32)
    relative = []
    for member in range(2):
        slice_sum = jnp.sum(maskf[member] * (label_list[member] - total_list[member]))
        relative.append((slice_sum + other_logps[member]) - ref_logps[member])
    margin = beta_value * (relative[0] - relative[1])
    coef = beta_value * jax.nn.sigmoid(-margin)
    seq_coefs = [-coef, coef]
    columns = jnp.arange(head_weight.shape[0], dtype=jnp.int32)
    grads_hidden = []
    grad_head = jnp.zeros(head_weight.shape, jnp.float32)
    for member in range(2):
        logits = logit_list[member]
        log_total = total_list[member]
        probs = jnp.exp(logits - log_total[:, None])
        onehot = (labels[member][:, None] == columns[None, :]).astype(jnp.float32)
        logit_grad = (loss_scale * maskf[member][:, None] * (seq_coefs[member] * (onehot - probs) + 2.0 * z_weight * log_total[:, None] * probs)).astype(jnp.bfloat16)
        grads_hidden.append(jnp.dot(logit_grad, head_weight, preferred_element_type=jnp.float32).astype(jnp.bfloat16))
        grad_head = grad_head + jnp.dot(logit_grad.T, hidden[member], preferred_element_type=jnp.float32)
    return jnp.stack(grads_hidden, axis=0), grad_head.astype(jnp.bfloat16)
```

```python
import jax
import jax.numpy as jnp
from jax import lax
from jax.experimental import pallas as pl
from jax.experimental.pallas import tpu as pltpu
from jax.sharding import Mesh, PartitionSpec as P

beta_value = 0.01
z_weight = 0.0001
loss_scale = 4096.0


SIZES = {"p": 2, "y": 4, "z": 8, "x": 4}
f32 = jnp.float32
bf16 = jnp.bfloat16


def shift(block, axis, by):
    n = SIZES[axis]
    return lax.ppermute(block, axis, [(i, (i + by) % n) for i in range(n)])


def take(array, index):
    return lax.dynamic_index_in_dim(array, index, 0, keepdims=False)


def ring_scatter(blocks, axis, relative):
    n = SIZES[axis]
    me = lax.axis_index(axis)

    def block(ahead):
        return blocks[ahead % n] if relative else take(blocks, (me + ahead) % n)

    half = n // 2
    far = block(half)
    cut = far.shape[0] // 2
    up, down = far[:cut].astype(bf16), far[cut:].astype(bf16)
    for step in range(1, half + 1):
        got_up, got_down = shift(up, axis, 1), shift(down, axis, -1)
        ahead = half - step
        if step == 1 and ahead > 0:
            a, b = block(ahead), block(-ahead)
            up = jnp.concatenate([a[:cut].astype(f32) + got_up.astype(f32), a[cut:].astype(f32)]).astype(bf16)
            down = jnp.concatenate([b[:cut].astype(f32), b[cut:].astype(f32) + got_down.astype(f32)]).astype(bf16)
        elif ahead > 0:
            up = (block(ahead).astype(f32) + got_up.astype(f32)).astype(bf16)
            down = (block(-ahead).astype(f32) + got_down.astype(f32)).astype(bf16)
    return block(0).astype(f32) + got_up.astype(f32) + got_down.astype(f32)


def terms_kernel(grad_ref, head_ref, first_ref, second_ref):
    for r in range(8):
        k, s = divmod(r, 2)
        out = jnp.dot(grad_ref[pl.ds(r * 128, 128), :], head_ref[...], preferred_element_type=f32).astype(bf16)
        for j in range(4):
            if s == 0:
                first_ref[j, k, 0] = out[:, j * 128 : (j + 1) * 128]
            else:
                second_ref[k, j, 0] = out[:, j * 128 : (j + 1) * 128]


def terms(grads, head):
    rows, inner = grads.shape
    return pl.pallas_call(
        terms_kernel,
        grid=(8,),
        in_specs=[
            pl.BlockSpec((rows, inner), lambda i: (0, 0)),
            pl.BlockSpec((inner, 512), lambda i: (0, i)),
        ],
        out_specs=[
            pl.BlockSpec((4, 4, 1, 128, 128), lambda i: (0, 0, i, 0, 0)),
            pl.BlockSpec((4, 4, 1, 128, 128), lambda i: (0, 0, i, 0, 0)),
        ],
        out_shape=[jax.ShapeDtypeStruct((4, 4, 8, 128, 128), bf16)] * 2,
        cost_estimate=pl.CostEstimate(flops=2 * rows * inner * 4096, bytes_accessed=14 << 20, transcendentals=0),
        name="terms",
    )(grads, head)


def turn(array, by):
    return lax.dynamic_slice_in_dim(jnp.concatenate([array, array[:3]]), by % 4, 4, 0)


def local(hidden, head, labels, token_mask, other_logps, ref_logps):
    p, y, z, x = (lax.axis_index(a) for a in "pyzx")
    own = lax.dynamic_slice_in_dim(hidden[0], p * 4096, 4096, 1)
    sent = lax.dynamic_slice_in_dim(hidden[0], (1 - p) * 4096, 4096, 1)
    mine = jnp.concatenate([own, shift(sent, "p", 1)])

    labels2 = jnp.concatenate([labels, shift(labels, "p", 1)])
    mask2 = jnp.concatenate([token_mask, shift(token_mask, "p", 1)])
    base = jnp.concatenate([other_logps, ref_logps])
    base2 = jnp.stack([base, shift(base, "p", 1)])

    strip = lax.dynamic_slice_in_dim(mine, x * 512, 512, 1)
    wide = mine[:, 2048:]
    strip_p, strip_m = shift(strip, "y", -1), shift(strip, "y", 1)
    wide_p, wide_m = shift(wide, "y", -1), shift(wide, "y", 1)
    strip_f = jnp.concatenate([shift(strip_p[:128], "y", -1), shift(strip_m[128:], "y", 1)])
    wide_f = jnp.concatenate([shift(wide_p[:128], "y", -1), shift(wide_m[128:], "y", 1)])
    foreign = jnp.stack([strip_p, strip_f, strip_m])
    from_p, from_m = shift(foreign, "x", -1), shift(foreign, "x", 1)
    from_f = jnp.concatenate([shift(from_p[:, :128], "x", -1), shift(from_m[:, 128:], "x", 1)], axis=1)
    rest = jnp.zeros((3, 256, 2048), bf16)
    for ahead, piece in enumerate((foreign, from_p, from_f, from_m)):
        rest = lax.dynamic_update_slice_in_dim(rest, piece, ((x + ahead) % 4) * 512, 2)
    rest = jnp.concatenate([rest, jnp.stack([wide_p, wide_f, wide_m])], axis=2)
    rows = jnp.concatenate([mine[None], rest]).reshape(1024, 4096)

    partial = lax.dot_general(rows, head, (((1,), (1,)), ((), ())), preferred_element_type=f32)
    partial = partial.reshape(4, 2, 128, 512)
    logits = partial + shift(partial, "p", 1)[:, ::-1]

    place = (y * 8 + z) * 4 + x
    columns = place * 512 + jnp.arange(512, dtype=jnp.int32)
    labels_abs = labels2.reshape(2, 4, 128).transpose(1, 0, 2)
    mask_abs = mask2.reshape(2, 4, 128).transpose(1, 0, 2).astype(f32)
    labels_rel, mask_rel = turn(labels_abs, y), turn(mask_abs, y)
    onehot = labels_rel[..., None] == columns
    top = jnp.max(logits, axis=-1)
    stats = jnp.stack([top, jnp.sum(jnp.exp(logits - top[..., None]), axis=-1), jnp.sum(jnp.where(onehot, logits, 0.0), axis=-1)], axis=1)
    stats = turn(stats, 4 - y)
    for axes, n in ((("z",), 8), (("y", "x"), 16)):
        got = lax.all_to_all(jnp.broadcast_to(stats[None], (n,) + stats.shape), axes, 0, 0, tiled=True)
        top = jnp.max(got[:, :, 0], axis=0)
        total = jnp.sum(got[:, :, 1] * jnp.exp(got[:, :, 0] - top), axis=0)
        stats = jnp.stack([top, total, jnp.sum(got[:, :, 2], axis=0)], axis=1)
    log_total = stats[:, 0] + jnp.log(stats[:, 1])
    slice_sum = jnp.sum(mask_abs * (stats[:, 2] - log_total), axis=(0, 2))
    relative = (slice_sum + base2[:, 0]) - base2[:, 1]
    margin = beta_value * jnp.where(p == 0, relative[0] - relative[1], relative[1] - relative[0])
    coef = beta_value * jax.nn.sigmoid(-margin)
    first = jnp.where(p == 0, -coef, coef)
    seq_coef = jnp.stack([first, -first])[None, :, None, None]
    log_rel = turn(log_total, y)[..., None]
    probs = jnp.exp(logits - log_rel)
    grads = (
        loss_scale * mask_rel[..., None] * (seq_coef * (onehot.astype(f32) - probs) + 2.0 * z_weight * log_rel * probs)
    ).astype(bf16)
    grads = grads.reshape(1024, 512)

    first, second = terms(grads, head)
    first = ring_scatter(first, "x", False)
    second = ring_scatter(second, "y", True)
    grad_head = lax.dot_general(grads, rows, (((0,), (0,)), ((), ())), preferred_element_type=f32).astype(bf16)
    first = ring_scatter(first, "y", True)
    second = ring_scatter(second, "x", False)
    both = ring_scatter(jnp.stack([first, second], axis=1), "z", False)
    grad_hidden = jnp.where(p == 0, both, both[::-1]).astype(bf16)
    return (grad_hidden, grad_head)


def solution(mesh):
    sub = Mesh(mesh.devices.reshape(2, 4, 8, 4), ("p", "y", "z", "x"))
    return jax.shard_map(
        local,
        mesh=sub,
        in_specs=(P("p", "y", None), P(("y", "z", "x"), "p"), P("p", None), P("p", None), P("p"), P("p")),
        out_specs=(P(None, "y", ("p", "z", "x")), P(("y", "z", "x"), "p")),
        check_vma=False,
    )
```

```python
import jax
import jax.numpy as jnp
from jax import lax
from jax.experimental import pallas as pl
from jax.experimental.pallas import tpu as pltpu
from jax.sharding import Mesh, PartitionSpec as P


beta_value = 0.01
z_weight = 0.0001
loss_scale = 4096.0


SIZES = {"p": 2, "y": 4, "z": 8, "x": 4}
f32 = jnp.float32
bf16 = jnp.bfloat16
CUT = 640


def shift(block, axis, by):
    n = SIZES[axis]
    return lax.ppermute(block, axis, [(i, (i + by) % n) for i in range(n)])


def turn(array, by, axis):
    twice = jnp.concatenate([array, lax.slice_in_dim(array, 0, 3, axis=axis)], axis=axis)
    return lax.dynamic_slice_in_dim(twice, by % 4, 4, axis)


def dot(a, b, dims):
    return lax.dot_general(a, b, (dims, ((), ())), preferred_element_type=f32)


def scatter4(far, near_up, near_down, own, axis, after=None):
    up = shift(far(0).astype(bf16), axis, 1)
    down = shift(far(1).astype(bf16), axis, -1)
    plain_up = shift(near_up(1).astype(bf16), axis, 1)
    plain_down = shift(near_down(0).astype(bf16), axis, -1)
    if after is not None:
        up, after = lax.optimization_barrier((up, after))
    up = shift((near_up(0) + up.astype(f32)).astype(bf16), axis, 1)
    down = shift((near_down(1) + down.astype(f32)).astype(bf16), axis, -1)
    return [own(0) + up.astype(f32) + plain_down.astype(f32), own(1) + down.astype(f32) + plain_up.astype(f32)], after


def scatter4_small(blocks, axis):
    b = blocks
    up = shift(jnp.stack([b[0][2], b[1][1]]).astype(bf16), axis, 1)
    down = shift(jnp.stack([b[1][2], b[0][3]]).astype(bf16), axis, -1)
    up2 = shift((b[0][1] + up[0].astype(f32)).astype(bf16), axis, 1)
    down2 = shift((b[1][3] + down[0].astype(f32)).astype(bf16), axis, -1)
    return [b[0][0] + up2.astype(f32) + down[1].astype(f32), b[1][0] + down2.astype(f32) + up[1].astype(f32)]


def scatter8(blocks, me, axis):
    twice = jnp.concatenate([blocks, blocks], axis=1)
    b = lax.dynamic_slice_in_dim(twice, me, 8, 1)
    up = jnp.stack([b[0, 4], b[1, 3]]).astype(bf16)
    down = jnp.stack([b[1, 4], b[0, 5]]).astype(bf16)
    for step in (1, 2):
        up, down = shift(up, axis, 1), shift(down, axis, -1)
        up = (jnp.stack([b[0, 4 - step], b[1, 3 - step]]) + up.astype(f32)).astype(bf16)
        down = (jnp.stack([b[1, 4 + step], b[0, 5 + step]]) + down.astype(f32)).astype(bf16)
    up, down = shift(up, axis, 1), shift(down, axis, -1)
    up2 = shift((b[0, 1] + up[0].astype(f32)).astype(bf16), axis, 1)
    down2 = shift((b[1, 7] + down[0].astype(f32)).astype(bf16), axis, -1)
    return jnp.stack([b[0, 0] + up2.astype(f32) + down[1].astype(f32), b[1, 0] + down2.astype(f32) + up[1].astype(f32)])


def order_kernel(x_ref, head_ref, out_ref):
    step = pl.program_id(0)
    for ahead in range(4):
        source = pl.multiple_of((x_ref[0] + ahead) % 4 * 128, 128)
        target = pl.multiple_of((step // 4 * 16 + ahead * 4 + step % 4) * 128, 128)
        out_ref[:, pl.ds(target, 128)] = head_ref[:, pl.ds(source, 128)]


def order_columns(head, x):
    return pl.pallas_call(
        order_kernel,
        grid_spec=pltpu.PrefetchScalarGridSpec(
            num_scalar_prefetch=1,
            grid=(8,),
            in_specs=[pl.BlockSpec((512, 512), lambda i, x_ref: (0, i))],
            out_specs=pl.BlockSpec((512, 4096), lambda i, x_ref: (0, 0)),
        ),
        out_shape=jax.ShapeDtypeStruct((512, 4096), bf16),
        cost_estimate=pl.CostEstimate(flops=0, bytes_accessed=8 << 20, transcendentals=0),
        compiler_params=pltpu.CompilerParams(vmem_limit_bytes=16 << 20),
        name="order_columns",
    )(x.astype(jnp.int32).reshape(1), head)


def local(hidden, head, labels, token_mask, other_logps, ref_logps):
    p, y, z, x = (lax.axis_index(a) for a in "pyzx")
    own = lax.dynamic_slice_in_dim(hidden, p * 4096, 4096, 2)
    sent = lax.dynamic_slice_in_dim(hidden, (1 - p) * 4096, 4096, 2)
    mine = jnp.concatenate([own, shift(sent, "p", 1)])

    labels2 = jnp.concatenate([labels, shift(labels, "p", 1)]).reshape(2, 4, 128)
    mask2 = jnp.concatenate([token_mask, shift(token_mask, "p", 1)]).reshape(2, 4, 128).astype(f32)
    base = jnp.concatenate([other_logps, ref_logps])
    base2 = jnp.stack([base, shift(base, "p", 1)])
    labels_rel, mask_rel = turn(labels2, y, 1).reshape(1024, 1), turn(mask2, y, 1).reshape(1024, 1)

    strip = lax.dynamic_slice_in_dim(mine, x * CUT, CUT, 2)
    strip_p, strip_m = shift(strip, "y", -1), shift(strip, "y", 1)
    wide = mine[:, :, 4 * CUT :]
    wide, head_in, strip_p, strip_m = lax.optimization_barrier((wide, head, strip_p, strip_m))
    strip_f0, strip_f1 = shift(strip_p[0], "y", -1), shift(strip_m[1], "y", 1)
    wide_p, wide_m = shift(wide, "y", -1), shift(wide, "y", 1)
    foreign = jnp.stack([strip_p[0], strip_f0, strip_m[0], strip_p[1], strip_f1, strip_m[1]])
    from_p, from_m = shift(foreign, "x", -1), shift(foreign, "x", 1)
    head_x = order_columns(head_in, x)
    heads = [lax.dynamic_slice_in_dim(head_in, ((x + a) % 4) * CUT, CUT, 1) for a in range(4)]
    near = dot(mine.reshape(256, 4096), head_in, ((1,), (1,)))
    from_p, from_m, head_x, near, *heads = lax.optimization_barrier((from_p, from_m, head_x, near, *heads))
    from_f = shift(from_p[:3], "x", -1), shift(from_m[3:], "x", 1)
    wide_f = shift(wide_p[0], "y", -1), shift(wide_m[1], "y", 1)

    def flat(block):
        return block.reshape(-1, block.shape[-1])

    def against(block, part):
        return dot(flat(block), part, ((1,), (1,)))

    head_wide = head_in[:, 4 * CUT :]
    strips = against(foreign, heads[0]) + against(from_p, heads[1]) + against(from_m, heads[3])
    with_p, with_m = against(wide_p, head_wide), against(wide_m, head_wide)
    strips, with_p, with_m = lax.optimization_barrier((strips, with_p, with_m))
    parts = []
    for s in range(2):
        far = strips[384 * s : 384 * s + 384] + against(from_f[s], heads[2])
        parts.append(
            jnp.concatenate(
                [
                    near[128 * s : 128 * s + 128],
                    far[:128] + with_p[128 * s : 128 * s + 128],
                    far[128:256] + against(wide_f[s], head_wide),
                    far[256:] + with_m[128 * s : 128 * s + 128],
                ]
            )
        )
    logits = jnp.concatenate([parts[0] + shift(parts[1], "p", 1), parts[1] + shift(parts[0], "p", 1)])

    rows = jnp.zeros((8, 128, 4096), bf16)
    for s in range(2):
        rows = lax.dynamic_update_slice(rows, mine[s : s + 1], (4 * s, 0, 0))
        for ahead, piece in ((0, foreign), (1, from_p), (3, from_m)):
            rows = lax.dynamic_update_slice(rows, piece[3 * s : 3 * s + 3], (4 * s + 1, 0, ((x + ahead) % 4) * CUT))
        rows = lax.dynamic_update_slice(rows, from_f[s], (4 * s + 1, 0, ((x + 2) % 4) * CUT))
        rows = lax.dynamic_update_slice(rows, jnp.stack([wide_p[s], wide_f[s], wide_m[s]]), (4 * s + 1, 0, 4 * CUT))
    rows = rows.reshape(1024, 4096)

    device = (y * 8 + z) * 4 + x
    columns = device * 512 + jnp.arange(512, dtype=jnp.int32)
    onehot = labels_rel == columns
    top = jnp.max(logits, axis=-1)
    stats = jnp.stack([top, jnp.sum(jnp.exp(logits - top[..., None]), axis=-1), jnp.sum(jnp.where(onehot, logits, 0.0), axis=-1)])
    stats = turn(stats.reshape(3, 2, 4, 128), 4 - y, 2).reshape(3, 8, 128)
    for axes, n in ((("z",), 8), (("y", "x"), 16)):
        got = lax.all_to_all(jnp.broadcast_to(stats[None], (n, 3, 8, 128)), axes, 0, 0, tiled=True)
        top = jnp.max(got[:, 0], axis=0)
        total = jnp.sum(got[:, 1] * jnp.exp(got[:, 0] - top), axis=0)
        stats = jnp.stack([top, total, jnp.sum(got[:, 2], axis=0)])
    log_total = (stats[0] + jnp.log(stats[1])).reshape(2, 4, 128)
    slice_sum = jnp.sum(mask2 * (stats[2].reshape(2, 4, 128) - log_total), axis=(1, 2))
    relative = (slice_sum + base2[:, 0]) - base2[:, 1]
    margin = beta_value * jnp.where(p == 0, relative[0] - relative[1], relative[1] - relative[0])
    coef = beta_value * jax.nn.sigmoid(-margin)
    first = jnp.where(p == 0, -coef, coef)
    seq_coef = jnp.where(jnp.arange(1024) < 512, first, -first)[:, None]
    log_rel = turn(log_total, y, 1).reshape(1024, 1)
    probs = jnp.exp(logits - log_rel)
    grads = (
        loss_scale * mask_rel * (seq_coef * (onehot.astype(f32) - probs) + 2.0 * z_weight * log_rel * probs)
    ).astype(bf16)

    def own_block(ahead):
        return lambda h: dot(grads[:512], head_x[:, (h * 4 + ahead) * 512 : (h * 4 + ahead + 1) * 512], ((1,), (0,)))

    def partner_block(k):
        return lambda h: dot(grads[512 + k * 128 : 640 + k * 128], head_x[:, h * 2048 : (h + 1) * 2048], ((1,), (0,)))

    first, late = scatter4(own_block(2), own_block(1), own_block(3), own_block(0), "x", grads)
    second, _ = scatter4(partner_block(2), partner_block(1), partner_block(3), partner_block(0), "y")
    grad_head = dot(late, rows, ((0,), (0,))).astype(bf16)
    first, second, grad_head = lax.optimization_barrier((first, second, grad_head))
    first = scatter4_small([[f[k * 128 : k * 128 + 128] for k in range(4)] for f in first], "y")
    second = scatter4_small([[f[:, a * 512 : a * 512 + 512] for a in range(4)] for f in second], "x")
    both = jnp.stack([jnp.stack([half[:, j * 128 : j * 128 + 128] for half in r for j in range(4)]) for r in (first, second)])
    both = scatter8(both, z, "z")
    grad_hidden = jnp.where(p == 0, both, both[::-1]).astype(bf16)
    return (grad_hidden, grad_head)


def solution(mesh):
    sub = Mesh(mesh.devices.reshape(2, 4, 8, 4), ("p", "y", "z", "x"))

    return jax.shard_map(
        local,
        mesh=sub,
        in_specs=(P("p", "y", None), P(("y", "z", "x"), "p"), P("p", None), P("p", None), P("p"), P("p")),
        out_specs=(P(None, "y", ("p", "z", "x")), P(("y", "z", "x"), "p")),
        check_vma=False,
    )
```

```python
import jax
import jax.numpy as jnp
from jax import lax
from jax.experimental import pallas as pl
from jax.experimental.pallas import tpu as pltpu
from jax.sharding import Mesh, PartitionSpec as P


beta_value = 0.01
z_weight = 0.0001
loss_scale = 4096.0


SIZES = {"p": 2, "y": 4, "z": 8, "x": 4}
f32 = jnp.float32
bf16 = jnp.bfloat16
CUT = 640


def shift(block, axis, by):
    n = SIZES[axis]
    return lax.ppermute(block, axis, [(i, (i + by) % n) for i in range(n)])


def turn(array, by, axis):
    twice = jnp.concatenate([array, lax.slice_in_dim(array, 0, 3, axis=axis)], axis=axis)
    return lax.dynamic_slice_in_dim(twice, by % 4, 4, axis)


def dot(a, b, dims):
    return lax.dot_general(a, b, (dims, ((), ())), preferred_element_type=f32)


def scatter4(up, down, near_up, near_down, own, axis, cut, after=None):
    up, down = shift(up, axis, 1), shift(down, axis, -1)
    if after is not None:
        up, down, after = lax.optimization_barrier((up, down, after))
    up, down = cut(up.astype(f32)), cut(down.astype(f32))
    up2 = shift((near_up() + up[1]).astype(bf16), axis, 1)
    down2 = shift((near_down() + down[0]).astype(bf16), axis, -1)
    lower, upper = cut(own())
    return [lower + up2.astype(f32) + down[1], upper + down2.astype(f32) + up[0]], after


def scatter4_small(blocks, axis):
    b = blocks
    up = shift(jnp.stack([b[0][2], b[1][1]]).astype(bf16), axis, 1)
    down = shift(jnp.stack([b[1][2], b[0][3]]).astype(bf16), axis, -1)
    up2 = shift((b[0][1] + up[0].astype(f32)).astype(bf16), axis, 1)
    down2 = shift((b[1][3] + down[0].astype(f32)).astype(bf16), axis, -1)
    return [b[0][0] + up2.astype(f32) + down[1].astype(f32), b[1][0] + down2.astype(f32) + up[1].astype(f32)]


def order_kernel(x_ref, head_ref, out_ref):
    step = pl.program_id(0)
    for ahead in range(4):
        source = pl.multiple_of((x_ref[0] + ahead) % 4 * 128, 128)
        target = pl.multiple_of((ahead * 8 + step) * 128, 128)
        out_ref[:, pl.ds(target, 128)] = head_ref[:, pl.ds(source, 128)]


def order_columns(head, x):
    return pl.pallas_call(
        order_kernel,
        grid_spec=pltpu.PrefetchScalarGridSpec(
            num_scalar_prefetch=1,
            grid=(8,),
            in_specs=[pl.BlockSpec((512, 512), lambda i, x_ref: (0, i))],
            out_specs=pl.BlockSpec((512, 4096), lambda i, x_ref: (0, 0)),
        ),
        out_shape=jax.ShapeDtypeStruct((512, 4096), bf16),
        cost_estimate=pl.CostEstimate(flops=0, bytes_accessed=8 << 20, transcendentals=0),
        compiler_params=pltpu.CompilerParams(vmem_limit_bytes=16 << 20),
        name="order_columns",
    )(x.astype(jnp.int32).reshape(1), head)


def local(hidden, head, labels, token_mask, other_logps, ref_logps):
    p, y, z, x = (lax.axis_index(a) for a in "pyzx")
    own = lax.dynamic_slice_in_dim(hidden, p * 4096, 4096, 2)
    sent = lax.dynamic_slice_in_dim(hidden, (1 - p) * 4096, 4096, 2)
    mine = jnp.concatenate([own, shift(sent, "p", 1)])

    small = jnp.concatenate([labels.astype(f32).reshape(4, 128), token_mask.astype(f32).reshape(4, 128), jnp.pad(jnp.stack([other_logps, ref_logps]), ((0, 0), (0, 127)))])
    small = jnp.stack([small, shift(small, "p", 1)])
    mask2, base2 = small[:, 4:8], small[:, 8:10, 0]
    labels_rel = turn(small[:, :4], y, 1).reshape(1024, 1).astype(jnp.int32)
    mask_rel = turn(mask2, y, 1).reshape(1024, 1)

    strip = lax.dynamic_slice_in_dim(mine, x * CUT, CUT, 2)
    strip_p, strip_m = shift(strip, "y", -1), shift(strip, "y", 1)
    wide = mine[:, :, 4 * CUT :]
    wide, head_in, labels_rel, mask_rel, base2, mask2, strip_p, strip_m = lax.optimization_barrier((wide, head, labels_rel, mask_rel, base2, mask2, strip_p, strip_m))
    strip_f0, strip_f1 = shift(strip_p[0], "y", -1), shift(strip_m[1], "y", 1)
    strip_f0, strip_f1 = lax.optimization_barrier((strip_f0, strip_f1))
    wide_p, wide_m = shift(wide, "y", -1), shift(wide, "y", 1)
    foreign = jnp.stack([strip_p[0], strip_f0, strip_m[0], strip_p[1], strip_f1, strip_m[1]])
    from_p, from_m = shift(foreign, "x", -1), shift(foreign, "x", 1)
    head_x = order_columns(head_in, x)
    head_in, head_x = lax.optimization_barrier((head_in, head_x))
    heads = [lax.dynamic_slice_in_dim(head_in, ((x + a) % 4) * CUT, CUT, 1) for a in range(4)]
    near = dot(mine.reshape(256, 4096), head_in, ((1,), (1,)))
    from_p, from_m, head_x, near, *heads = lax.optimization_barrier((from_p, from_m, head_x, near, *heads))
    from_f = shift(from_p[:3], "x", -1), shift(from_m[3:], "x", 1)
    from_f = lax.optimization_barrier(from_f)
    wide_f = lax.optimization_barrier((shift(wide_p[0], "y", -1), shift(wide_m[1], "y", 1)))

    def flat(block):
        return block.reshape(-1, block.shape[-1])

    def against(block, part):
        return dot(flat(block), part, ((1,), (1,)))

    head_wide = head_in[:, 4 * CUT :]
    strips = against(foreign, heads[0]) + against(from_p, heads[1]) + against(from_m, heads[3])
    with_p, with_m = against(wide_p, head_wide), against(wide_m, head_wide)
    strips, with_p, with_m = lax.optimization_barrier((strips, with_p, with_m))
    parts = []
    for s in range(2):
        far = strips[384 * s : 384 * s + 384] + against(from_f[s], heads[2])
        parts.append(
            jnp.concatenate(
                [
                    near[128 * s : 128 * s + 128],
                    far[:128] + with_p[128 * s : 128 * s + 128],
                    far[128:256] + against(wide_f[s], head_wide),
                    far[256:] + with_m[128 * s : 128 * s + 128],
                ]
            )
        )
    both = jnp.stack(parts)
    logits = (both + shift(both, "p", 1)[::-1]).reshape(1024, 512)

    device = (y * 8 + z) * 4 + x
    columns = device * 512 + jnp.arange(512, dtype=jnp.int32)
    onehot = labels_rel == columns
    top = jnp.max(logits, axis=-1)
    stats = jnp.stack([top, jnp.sum(jnp.exp(logits - top[..., None]), axis=-1), jnp.sum(jnp.where(onehot, logits, 0.0), axis=-1)])
    stats = turn(stats.reshape(3, 2, 4, 128), 4 - y, 2).reshape(3, 8, 128)
    stats, mine, foreign, from_p, from_m, from_f, wide_p, wide_f, wide_m = lax.optimization_barrier(
        (stats, mine, foreign, from_p, from_m, from_f, wide_p, wide_f, wide_m)
    )
    rows = jnp.zeros((8, 128, 4096), bf16)
    for s in range(2):
        rows = lax.dynamic_update_slice(rows, mine[s : s + 1], (4 * s, 0, 0))
    for axes, n in ((("z",), 8), (("y", "x"), 16)):
        got = lax.all_to_all(jnp.broadcast_to(stats[None], (n, 3, 8, 128)), axes, 0, 0, tiled=True)
        top = jnp.max(got[:, 0], axis=0)
        total = jnp.sum(got[:, 1] * jnp.exp(got[:, 0] - top), axis=0)
        stats = jnp.stack([top, total, jnp.sum(got[:, 2], axis=0)])
    log_total = (stats[0] + jnp.log(stats[1])).reshape(2, 4, 128)
    slice_sum = jnp.sum(mask2 * (stats[2].reshape(2, 4, 128) - log_total), axis=(1, 2))
    relative = (slice_sum + base2[:, 0]) - base2[:, 1]
    margin = beta_value * jnp.where(p == 0, relative[0] - relative[1], relative[1] - relative[0])
    coef = beta_value * jax.nn.sigmoid(-margin)
    first = jnp.where(p == 0, -coef, coef)
    seq_coef = jnp.where(jnp.arange(1024) < 512, first, -first)[:, None]
    log_rel = turn(log_total, y, 1).reshape(1024, 1)
    probs = jnp.exp(logits - log_rel)
    grads = (
        loss_scale * mask_rel * (seq_coef * (onehot.astype(f32) - probs) + 2.0 * z_weight * log_rel * probs)
    ).astype(bf16)

    rows, grads, from_p, from_m, from_f, foreign, wide_p, wide_f, wide_m = lax.optimization_barrier(
        (rows, grads, from_p, from_m, from_f, foreign, wide_p, wide_f, wide_m)
    )
    for s in range(2):
        for ahead, piece in ((0, foreign[3 * s : 3 * s + 3]), (1, from_p[3 * s : 3 * s + 3]), (3, from_m[3 * s : 3 * s + 3]), (2, from_f[s])):
            rows = lax.dynamic_update_slice(rows, piece, (4 * s + 1, 0, ((x + ahead) % 4) * CUT))
        for k, piece in ((1, wide_p[s : s + 1]), (2, wide_f[s][None]), (3, wide_m[s : s + 1])):
            rows = lax.dynamic_update_slice(rows, piece, (4 * s + k, 0, 4 * CUT))
    rows = rows.reshape(1024, 4096)
    own_grads, partner_grads = grads[:512], grads[512:]

    def own_terms(start, stop):
        return dot(own_grads, head_x[:, start:stop], ((1,), (0,)))

    def partner_terms(start, stop):
        return dot(partner_grads[start:stop], head_x, ((1,), (0,)))

    first, late = scatter4(
        own_terms(1536, 2560).astype(bf16),
        own_terms(2560, 3584).astype(bf16),
        lambda: own_terms(1024, 1536),
        lambda: own_terms(3584, 4096),
        lambda: own_terms(0, 1024),
        "x",
        lambda r: (r[:, :512], r[:, 512:]),
        grads,
    )
    second, _ = scatter4(
        partner_terms(192, 320).astype(bf16),
        partner_terms(320, 448).astype(bf16),
        lambda: partner_terms(128, 192),
        lambda: partner_terms(448, 512),
        lambda: partner_terms(0, 128),
        "y",
        lambda r: (r[:64], r[64:]),
    )
    grad_head = dot(late, rows, ((0,), (0,))).astype(bf16)
    first, second, grad_head = lax.optimization_barrier((first, second, grad_head))
    second = jnp.stack([jnp.concatenate([f[:, a * 1024 : a * 1024 + 1024] for f in second]) for a in range(4)]).astype(bf16)
    second = lax.all_to_all(turn(second, 4 - x, 0), "x", 0, 0, tiled=True)
    first = scatter4_small([[f[k * 128 : k * 128 + 128] for k in range(4)] for f in first], "y")
    first, second = lax.optimization_barrier((first, second))
    second = jnp.sum(second.astype(f32), axis=0).astype(bf16)
    first = jnp.concatenate(first, axis=1).astype(bf16)
    both = jnp.stack([jnp.stack([r[:, j * 128 : j * 128 + 128] for r in (first, second)]) for j in range(8)])
    both = jnp.sum(lax.all_to_all(both, "z", 0, 0, tiled=True).astype(f32), axis=0)
    grad_hidden = jnp.where(p == 0, both, both[::-1]).astype(bf16)
    return (grad_hidden, grad_head)


def solution(mesh):
    sub = Mesh(mesh.devices.reshape(2, 4, 8, 4), ("p", "y", "z", "x"))

    return jax.shard_map(
        local,
        mesh=sub,
        in_specs=(P("p", "y", None), P(("y", "z", "x"), "p"), P("p", None), P("p", None), P("p"), P("p")),
        out_specs=(P(None, "y", ("p", "z", "x")), P(("y", "z", "x"), "p")),
        check_vma=False,
    )
```
